32 devices in a mesh: loop: 4 (over x, core), grp: 8 (over z, y).
Axes of the slice: x: 2, y: 2, z: 4, core: 2. Of those that a mesh axis runs over, the one named last changes fastest.
Arguments:
- basis: bfloat16 [24576, 256], P(('loop', 'grp')), may hold values from -6 to 6
- stiffness: bfloat16 [384, 16, 4096], P(('loop', 'grp')), may hold values from -0.1875 to 0.1875
- mass: bfloat16 [384, 16, 4096], P(('loop', 'grp')), may hold values from -0.1875 to 0.1875
- col_index: int32 [384, 16], P(('loop', 'grp')), may hold values from 0 to 11
- live_counts: int32 [384], P(('loop', 'grp')), may hold values from 1 to 16, as said below
Outputs:
- stiff_basis: bfloat16 [24576, 256], P(('loop', 'grp'))
- mass_basis: bfloat16 [24576, 256], P(('loop', 'grp'))
- stiff_gram: float32 [256, 256], replicated
- mass_gram: float32 [256, 256], replicated
The draws below stay inside these ranges and needn't reach their ends.
Inputs may be any that keep to these rules, and one draw needn't show every extreme that they name: `live_counts`: every block row keeps at least one block; some block row uses all 16 and some only one.
All inputs are finite; a program needn't handle non-finite values.
Results may differ from the reference program's by a relative error of at most 0.0029.
Values may be sent and summed in bfloat16 or wider, within the bound.
A program may use at most 64 MiB of HBM per device.

```python
import jax
import jax.numpy as jnp
from jax import lax

BS = 64
NB = 16
W = 256
BR_DEV = 12
NBR = 384
NDOF = 24576
N_LOOP = 4
N_GRP = 8


def draw_live_counts(key, part):
    counts = jax.random.randint(key, (NBR,), 1, NB + 1, dtype=jnp.int32)
    counts = counts.at[0].set(NB)
    counts = counts.at[1].set(1)
    return counts


def touch_ends(drawn, rng, smallest, top_value):
    longest = drawn.shape.index(max(drawn.shape))
    spots = []
    for shift in (0, 1):
        where = [jax.random.randint(jax.random.fold_in(rng, axis), (), 0, length) for axis, length in enumerate(drawn.shape)]
        where[longest] = (where[longest] + shift) % drawn.shape[longest]
        spots.append(tuple(where))
    return drawn.at[spots[0]].set(smallest).at[spots[1]].set(top_value)


def block_levels(rng, dims, pieces, smallest, top_value):
    level = 1.0
    for dim, shards_of in pieces:
        draws = jax.random.uniform(jax.random.fold_in(jax.random.fold_in(rng, 6), dim), (shards_of,), jnp.float32, smallest / len(pieces), top_value / len(pieces))
        level = level * jnp.repeat(jnp.exp(draws), dims[dim] // shards_of).reshape((-1,) + (1,) * (len(dims) - 1 - dim))
    return level


def centred(rng, extent, deviation, most, shards=(), kind=jnp.bfloat16):
    entries = deviation * jax.random.normal(rng, extent, jnp.float32)
    if shards:
        entries = entries * block_levels(rng, extent, shards, -0.22, 0.18)
    return jnp.clip(entries, -most, most).astype(kind)


def setup_inputs(seed: int = 0) -> dict:
    streams_of = jax.random.split(jax.random.key(seed), 6)
    basis = centred(streams_of[0], (NDOF, W), 1.0, 6.0, ((0, 32),))
    stiffness = centred(streams_of[1], (NBR, NB, BS * BS), (NB * BS) ** -0.5, 0.1875, ((0, 32),))
    mass = centred(streams_of[2], (NBR, NB, BS * BS), (NB * BS) ** -0.5, 0.1875, ((0, 32),))
    col_index = touch_ends(jax.random.randint(streams_of[3], (NBR, NB), 0, BR_DEV), jax.random.fold_in(streams_of[3], 1), 0, BR_DEV - 1).astype(jnp.int32)
    live_counts = draw_live_counts(jax.random.fold_in(streams_of[5], 71), 0)
    return dict(basis=basis, stiffness=stiffness, mass=mass, col_index=col_index, live_counts=live_counts)


slot_offsets = (0, 0, 0, 0, 0, 0, 1, 1, 1, -1, -1, -1, 2, 2, -2, -2)

def reference(basis, stiffness, mass, col_index, live_counts):
    ndev = N_LOOP * N_GRP
    blocks = basis.reshape(NBR, BS, W)
    slots = jnp.arange(NB, dtype=jnp.int32)
    offsets = jnp.array(slot_offsets, dtype=jnp.int32)

    def one_device(dev):
        start = (dev * BR_DEV).astype(jnp.int32)
        kb = lax.dynamic_slice_in_dim(stiffness, start, BR_DEV, 0).reshape(BR_DEV, NB, BS, BS)
        mb = lax.dynamic_slice_in_dim(mass, start, BR_DEV, 0).reshape(BR_DEV, NB, BS, BS)
        cidx = lax.dynamic_slice_in_dim(col_index, start, BR_DEV, 0)
        cnt = lax.dynamic_slice_in_dim(live_counts, start, BR_DEV, 0)
        loop_id = dev // N_GRP
        grp_id = dev % N_GRP
        owner = ((loop_id + offsets) % N_LOOP * N_GRP + grp_id).astype(jnp.int32)
        colblk = (owner[None, :] * BR_DEV + cidx).astype(jnp.int32)
        picked = blocks[colblk].astype(jnp.float32)
        live = (slots[None, :] < cnt[:, None]).astype(jnp.float32)
        picked = picked * live[:, :, None, None]
        kacc = jnp.einsum('rsab,rsbc->rac', kb.astype(jnp.float32), picked)
        macc = jnp.einsum('rsab,rsbc->rac', mb.astype(jnp.float32), picked)
        return (kacc.astype(jnp.bfloat16), macc.astype(jnp.bfloat16))
    kout, mout = lax.map(one_device, jnp.arange(ndev, dtype=jnp.int32))
    stiff_basis = kout.reshape(NDOF, W)
    mass_basis = mout.reshape(NDOF, W)
    factor = jnp.float32(1.0) / jnp.sqrt(jnp.float32(NDOF))
    stiff_gram = jnp.dot(basis.T, stiff_basis, preferred_element_type=jnp.float32) * factor
    mass_gram = jnp.dot(basis.T, mass_basis, preferred_element_type=jnp.float32) * factor
    return (stiff_basis, mass_basis, stiff_gram, mass_gram)
```

```python
import functools

import jax
import jax.numpy as jnp
from jax import lax
from jax.experimental import pallas as pl
from jax.experimental.pallas import tpu as pltpu
from jax.sharding import PartitionSpec as P

BS = 64
NB = 16


panel_spans = ((0, 0, 6), (1, 6, 3), (-1, 9, 3), (2, 12, 2), (-2, 14, 2))


def shifted(block, axis, distance):
    devices = range(lax.axis_size(axis))
    route = [((i - distance) % len(devices), i) for i in devices]
    return lax.ppermute(block, axis, route)


MESH = pl.DeviceIdType.MESH


def greet(nl, ng):
    me_l, me_g = lax.axis_index("loop"), lax.axis_index("grp")
    barrier = pltpu.get_barrier_semaphore()
    for d in range(1, nl):
        pl.semaphore_signal(barrier, inc=1, device_id=(lax.rem(me_l + d, nl), me_g), device_id_type=MESH)
    for d in range(1, ng):
        pl.semaphore_signal(barrier, inc=1, device_id=(me_l, lax.rem(me_g + d, ng)), device_id_type=MESH)
    pl.semaphore_wait(barrier, nl + ng - 2)


def reduce_all(nl, ng, split, factor, part, land_l, red, land_g, res, sems):
    me_l, me_g = lax.axis_index("loop"), lax.axis_index("grp")
    send_a, recv_a, send_b, recv_b, send_c, recv_c, send_d, recv_d = sems

    def to_loop(src, dst, send, recv, d):
        return pltpu.make_async_remote_copy(
            src_ref=src, dst_ref=dst, send_sem=send.at[d - 1], recv_sem=recv.at[d - 1],
            device_id=(lax.rem(me_l + d, nl), me_g), device_id_type=MESH)

    def to_grp(src, dst, send, recv, d):
        return pltpu.make_async_remote_copy(
            src_ref=src, dst_ref=dst, send_sem=send.at[d - 1], recv_sem=recv.at[d - 1],
            device_id=(me_l, lax.rem(me_g + d, ng)), device_id_type=MESH)

    copies = [to_loop(part.at[lax.rem(me_l + d, nl)], land_l.at[d - 1], send_a, recv_a, d) for d in range(1, nl)]
    for c in copies:
        c.start()
    for c in copies:
        c.wait()
    total = part[me_l]
    for d in range(1, nl):
        total = total + land_l[d - 1]
    red[...] = total
    whole = split == 1
    copies = [
        to_grp(red.at[0] if whole else red.at[lax.rem(me_g + d, ng)], land_g.at[d - 1], send_b, recv_b, d)
        for d in range(1, ng)
    ]
    for c in copies:
        c.start()
    for c in copies:
        c.wait()
    if whole:
        land_g[ng - 1] = red[0]
        mine = land_g[lax.rem(me_g + ng - 1, ng)]
        for g in range(1, ng):
            mine = mine + land_g[lax.rem(me_g - g + 2 * ng - 1, ng)]
        res[me_l, 0] = mine * factor
    else:
        mine = red[me_g]
        for d in range(1, ng):
            mine = mine + land_g[d - 1]
        res[me_l, me_g] = mine * factor
        piece = res.at[me_l, me_g]
        copies = [to_grp(piece, piece, send_c, recv_c, d) for d in range(1, ng)]
        for c in copies:
            c.start()
        for c in copies:
            c.wait()
    piece = res.at[me_l]
    copies = [to_loop(piece, piece, send_d, recv_d, d) for d in range(1, nl)]
    for c in copies:
        c.start()
    for c in copies:
        c.wait()


def reduce_kernel(nl, ng, split, factor, part, res, land_l, red, land_g, *sems):
    greet(nl, ng)
    reduce_all(nl, ng, split, factor, part, land_l, red, land_g, res, sems)


def all_reduce(kterm, mterm, factor):
    nl, ng = lax.axis_size("loop"), lax.axis_size("grp")
    width = kterm.shape[1]
    rows = 2 * kterm.shape[0] // nl
    split = ng if rows % (8 * ng) == 0 else 1
    rows = rows // split
    part = jnp.concatenate([kterm, mterm], 0).reshape(nl, split, rows, width)
    f32 = jnp.float32
    vm = pl.BlockSpec(memory_space=pltpu.VMEM)
    sem = pltpu.SemaphoreType.DMA
    out = pl.pallas_call(
        functools.partial(reduce_kernel, nl, ng, split, factor),
        out_shape=jax.ShapeDtypeStruct(part.shape, f32),
        in_specs=[vm],
        out_specs=vm,
        scratch_shapes=[
            pltpu.VMEM((nl - 1, split, rows, width), f32),
            pltpu.VMEM((split, rows, width), f32),
            pltpu.VMEM((ng, rows, width), f32),
        ] + [sem((n - 1,)) for n in (nl, nl, ng, ng, ng, ng, nl, nl)],
        compiler_params=pltpu.CompilerParams(collective_id=0, has_side_effects=True),
    )(part)
    out = out.reshape(2, kterm.shape[0], width)
    return out[0], out[1]


def on_device(basis, stiffness, mass, col_index, live_counts):
    rows_dev = stiffness.shape[0]
    width = basis.shape[1]
    kb = stiffness.reshape(rows_dev, NB, BS, BS)
    mb = mass.reshape(rows_dev, NB, BS, BS)
    slot_ids = jnp.arange(NB, dtype=jnp.int32)
    live_grid = slot_ids[None, :] < live_counts[:, None]
    panels = {
        0: basis,
        1: shifted(basis, "loop", -1),
        -1: shifted(basis, "loop", 1),
        2: shifted(basis, "loop", -2),
        -2: shifted(basis, "loop", 2),
    }
    zeros_acc = jnp.zeros((rows_dev, BS, width), jnp.float32)
    accs = (zeros_acc, zeros_acc)
    for shift_by, first, count in panel_spans:
        blocks = panels[shift_by].reshape(rows_dev, BS, width)
        chosen = col_index[:, first : first + count]
        alive = live_grid[:, first : first + count]
        picked = blocks[chosen]
        picked = jnp.where(alive[:, :, None, None], picked, jnp.zeros_like(picked))
        kadd = jnp.einsum(
            "rjab,rjbc->rac",
            kb[:, first : first + count],
            picked,
            preferred_element_type=jnp.float32,
        )
        madd = jnp.einsum(
            "rjab,rjbc->rac",
            mb[:, first : first + count],
            picked,
            preferred_element_type=jnp.float32,
        )
        accs = (accs[0] + kadd, accs[1] + madd)
    kacc, macc = accs
    stiff_basis = kacc.reshape(rows_dev * BS, width).astype(jnp.bfloat16)
    mass_basis = macc.reshape(rows_dev * BS, width).astype(jnp.bfloat16)
    contract = (((0,), (0,)), ((), ()))
    kterm = lax.dot_general(basis, stiff_basis, contract, preferred_element_type=jnp.float32)
    mterm = lax.dot_general(basis, mass_basis, contract, preferred_element_type=jnp.float32)
    total_dofs = basis.shape[0] * lax.axis_size("loop") * lax.axis_size("grp")
    kgram, mgram = all_reduce(kterm, mterm, 1.0 / total_dofs**0.5)
    return (stiff_basis, mass_basis, kgram, mgram)


def solution(mesh):
    in_specs = (
        P(("loop", "grp"), None),
        P(("loop", "grp"), None, None),
        P(("loop", "grp"), None, None),
        P(("loop", "grp"), None),
        P(("loop", "grp")),
    )
    out_specs = (P(("loop", "grp"), None), P(("loop", "grp"), None), P(), P())
    return jax.shard_map(
        on_device, mesh=mesh, in_specs=in_specs, out_specs=out_specs, check_vma=False
    )
```

```python
import functools

import jax
import jax.numpy as jnp
from jax import lax
from jax.experimental import pallas as pl
from jax.experimental.pallas import tpu as pltpu
from jax.sharding import PartitionSpec as P

BS = 64
NB = 16
LOCAL = 6
LANES = 128
GROUPS = 4
MESH = pl.DeviceIdType.MESH
BF16 = jnp.bfloat16
F32 = jnp.float32

SIB, AHEAD, FWD, BEHIND = range(4)


def fused_kernel(
    nl, ng, split, factor,
    col, live, basis, k_hbm, m_hbm,
    sbk, sbm, kgram, mgram,
    k_raw, m_raw, k_scr, m_scr, lhs, own, panels, basis_t, acc, tmp,
    part, land_c, half, land_q, red, land_g, res,
    own_sem, k_sem, m_sem, s_sib, r_sib, s_ahead, r_ahead, s_behind, r_behind, s_fwd, r_fwd,
    s_a1, r_a1, s_a2, r_a2, s_b, r_b, s_c, r_c, s_d1, r_d1, s_d2, r_d2,
):
    me_l, me_g = lax.axis_index("loop"), lax.axis_index("grp")
    nq = nl // 2
    me_q, me_c = me_l // 2, lax.rem(me_l, 2)
    n_rows = k_raw.shape[0]
    width = basis.shape[2]
    per = n_rows // GROUPS
    sibling = (2 * me_q + 1 - me_c, me_g)

    def chip(d):
        return (2 * lax.rem(me_q + d, nq) + me_c, me_g)

    def grp(d):
        return (me_l, lax.rem(me_g + d, ng))

    def send(src, dst, s, r, dev):
        return pltpu.make_async_remote_copy(
            src_ref=src, dst_ref=dst, send_sem=s, recv_sem=r, device_id=dev, device_id_type=MESH)

    own_load = pltpu.make_async_copy(basis, own.at[pl.ds(0, n_rows)], own_sem)
    own_load.start()
    loads = []
    for t in range(GROUPS):
        span = pl.ds(t * per, per)
        pair = (
            pltpu.make_async_copy(k_hbm.at[span], k_raw.at[span], k_sem.at[t]),
            pltpu.make_async_copy(m_hbm.at[span], m_raw.at[span], m_sem.at[t]),
        )
        for c in pair:
            c.start()
        loads.append(pair)

    barrier = pltpu.get_barrier_semaphore()
    pl.semaphore_signal(barrier, inc=1, device_id=sibling, device_id_type=MESH)
    for d in range(1, nq):
        pl.semaphore_signal(barrier, inc=1, device_id=chip(d), device_id_type=MESH)
    for d in range(1, ng):
        pl.semaphore_signal(barrier, inc=1, device_id=grp(d), device_id_type=MESH)
    pl.semaphore_wait(barrier, 1 + (nq - 1) + (ng - 1))

    two_ways = nq > 2
    ahead, behind, forward = [], [], []
    far = AHEAD if not two_ways else jnp.where(me_c == 0, AHEAD, BEHIND)
    for t in range(GROUPS):
        span = pl.ds(t * per, per)
        c = send(basis.at[span], panels.at[AHEAD, span], s_ahead.at[t], r_ahead.at[t], chip(nq - 1))
        c.start()
        ahead.append(c)
        if two_ways:
            c = send(basis.at[span], panels.at[BEHIND, span], s_behind.at[t], r_behind.at[t], chip(1))
            c.start()
            behind.append(c)
        forward.append(send(panels.at[far, span], panels.at[FWD, span], s_fwd.at[t], r_fwd.at[t], sibling))
    sib = send(basis, panels.at[SIB, pl.ds(0, n_rows)], s_sib, r_sib, sibling)
    sib.start()

    own[n_rows] = jnp.zeros((BS, width), BF16)
    for s in range(panels.shape[0]):
        panels[s, n_rows] = jnp.zeros((BS, width), BF16)

    low = lax.broadcasted_iota(jnp.int32, (BS // 2, LANES), 1) < BS

    def relayout(raw, scr, r, base):
        for p in range(BS // 2):
            scr[p * NB : (p + 1) * NB, :] = raw[r, :, p * LANES : (p + 1) * LANES].astype(F32)
        for j in range(NB // 2):
            even = scr[pl.ds(2 * j, BS // 2, stride=NB), :]
            odd = scr[pl.ds(2 * j + 1, BS // 2, stride=NB), :]
            first = jnp.where(low, even, pltpu.roll(odd, BS, 1))
            second = jnp.where(low, pltpu.roll(even, BS, 1), odd)
            lanes = slice(j * LANES, (j + 1) * LANES)
            lhs[r, base : base + BS // 2, lanes] = first.astype(BF16)
            lhs[r, base + BS // 2 : base + BS, lanes] = second.astype(BF16)

    for t in range(GROUPS):
        for c in loads[t]:
            c.wait()

        def rows(r, carry):
            relayout(k_raw, k_scr, r, 0)
            relayout(m_raw, m_scr, r, BS)
            return carry

        lax.fori_loop(t * per, (t + 1) * per, rows, 0)
        ahead[t].wait_recv()
        if two_ways:
            behind[t].wait_recv()
        forward[t].start()

    def block(r, s):
        return jnp.where(s < live[r], col[r, s], n_rows)

    own_load.wait()

    def local_rows(r, carry):
        rhs = jnp.concatenate([own[block(r, s)] for s in range(LOCAL)], 0)
        acc[r] = jnp.dot(lhs[r, :, : LOCAL * BS], rhs, preferred_element_type=F32)
        return carry

    lax.fori_loop(0, n_rows, local_rows, 0)
    basis_t[...] = own[:n_rows].reshape(n_rows * BS, width).T

    sib.wait()
    for t in range(GROUPS):
        ahead[t].wait_send()
        if two_ways:
            behind[t].wait_send()
        forward[t].wait()

    plus = jnp.where(me_c == 0, SIB, FWD)
    minus = jnp.where(me_c == 0, FWD, SIB)
    back = BEHIND if two_ways else AHEAD
    owners = [plus] * 3 + [minus] * 3 + [AHEAD] * 2 + [back] * 2

    def remote_rows(r, carry):
        rhs = jnp.concatenate([panels[o, block(r, LOCAL + s)] for s, o in enumerate(owners)], 0)
        out = acc[r] + jnp.dot(lhs[r, :, LOCAL * BS :], rhs, preferred_element_type=F32)
        h = BS // 2
        for m, dst in enumerate((sbk, sbm)):
            for w in range(width // LANES):
                i = m * (width // LANES) + w
                lanes = slice(w * LANES, (w + 1) * LANES)
                tmp[i, pl.ds(0, h, stride=2), :] = out[m * BS : m * BS + h, lanes]
                tmp[i, pl.ds(1, h, stride=2), :] = out[m * BS + h : (m + 1) * BS, lanes]
                dst[r, :, lanes] = tmp[i].astype(BF16)
        return carry

    lax.fori_loop(0, n_rows, remote_rows, 0)

    step = part.shape[3]
    pieces = width // step
    for m, src in enumerate((sbk, sbm)):
        gram = jnp.dot(basis_t[...], src[...].reshape(n_rows * BS, width), preferred_element_type=F32)
        for i in range(pieces):
            n = m * pieces + i
            part[n // (2 * split), n // split % 2, n % split] = gram[i * step : (i + 1) * step]

    c = send(part.at[:, 1 - me_c], land_c, s_a1, r_a1, sibling)
    c.start()
    c.wait()
    half[...] = part[:, me_c] + land_c[...]
    copies = [
        send(half.at[lax.rem(me_q + d, nq)], land_q.at[d - 1], s_a2.at[d - 1], r_a2.at[d - 1], chip(d))
        for d in range(1, nq)
    ]
    for c in copies:
        c.start()
    for c in copies:
        c.wait()
    total = half[me_q]
    for d in range(1, nq):
        total = total + land_q[d - 1]
    red[...] = total
    whole = split == 1
    copies = [
        send(red.at[0] if whole else red.at[lax.rem(me_g + d, ng)], land_g.at[d - 1], s_b.at[d - 1], r_b.at[d - 1], grp(d))
        for d in range(1, ng)
    ]
    for c in copies:
        c.start()
    for c in copies:
        c.wait()
    if whole:
        land_g[ng - 1] = red[0]
        mine = land_g[lax.rem(me_g + ng - 1, ng)]
        for g in range(1, ng):
            mine = mine + land_g[lax.rem(me_g - g + 2 * ng - 1, ng)]
        res[me_q, me_c, 0] = mine * factor
    else:
        mine = red[me_g]
        for d in range(1, ng):
            mine = mine + land_g[d - 1]
        res[me_q, me_c, me_g] = mine * factor
        piece = res.at[me_q, me_c, me_g]
        copies = [send(piece, piece, s_c.at[d - 1], r_c.at[d - 1], grp(d)) for d in range(1, ng)]
        for c in copies:
            c.start()
        for c in copies:
            c.wait()
    piece = res.at[me_q, me_c]
    copies = [send(piece, piece, s_d1.at[d - 1], r_d1.at[d - 1], chip(d)) for d in range(1, nq)]
    for c in copies:
        c.start()
    for c in copies:
        c.wait()
    piece = res.at[:, me_c]
    c = send(piece, piece, s_d2, r_d2, sibling)
    c.start()
    c.wait()
    for m, dst in enumerate((kgram, mgram)):
        for i in range(pieces):
            n = m * pieces + i
            dst[i * step : (i + 1) * step, :] = res[n // (2 * split), n // split % 2, n % split]


def on_device(basis, stiffness, mass, col_index, live_counts):
    nl, ng = lax.axis_size("loop"), lax.axis_size("grp")
    nq = nl // 2
    n_rows = stiffness.shape[0]
    width = basis.shape[1]
    step = 2 * width // nl
    split = ng if step % (8 * ng) == 0 else 1
    step = step // split
    factor = 1.0 / (basis.shape[0] * nl * ng) ** 0.5
    vmem, smem, hbm = (pl.BlockSpec(memory_space=s) for s in (pltpu.VMEM, pltpu.SMEM, pltpu.HBM))
    sem = pltpu.SemaphoreType.DMA
    sb = jax.ShapeDtypeStruct((n_rows, BS, width), BF16)
    gram = jax.ShapeDtypeStruct((width, width), F32)
    stiff, massb, kgram, mgram = pl.pallas_call(
        functools.partial(fused_kernel, nl, ng, split, factor),
        out_shape=(sb, sb, gram, gram),
        in_specs=[smem, smem, hbm, hbm, hbm],
        out_specs=(vmem,) * 4,
        scratch_shapes=[
            pltpu.VMEM(stiffness.shape, BF16),
            pltpu.VMEM(mass.shape, BF16),
            pltpu.VMEM((NB * BS // 2, LANES), F32),
            pltpu.VMEM((NB * BS // 2, LANES), F32),
            pltpu.VMEM((n_rows, 2 * BS, NB * BS), BF16),
            pltpu.VMEM((n_rows + 1, BS, width), BF16),
            pltpu.VMEM((4 if nq > 2 else 3, n_rows + 1, BS, width), BF16),
            pltpu.VMEM((width, n_rows * BS), BF16),
            pltpu.VMEM((n_rows, 2 * BS, width), F32),
            pltpu.VMEM((2 * width // LANES, BS, LANES), F32),
            pltpu.VMEM((nq, 2, split, step, width), F32),
            pltpu.VMEM((nq, split, step, width), F32),
            pltpu.VMEM((nq, split, step, width), F32),
            pltpu.VMEM((nq - 1, split, step, width), F32),
            pltpu.VMEM((split, step, width), F32),
            pltpu.VMEM((ng, step, width), F32),
            pltpu.VMEM((nq, 2, split, step, width), F32),
            sem(()), sem((GROUPS,)), sem((GROUPS,)), sem(()), sem(()),
            sem((GROUPS,)), sem((GROUPS,)), sem((GROUPS,)), sem((GROUPS,)), sem((GROUPS,)), sem((GROUPS,)),
            sem(()), sem(()), sem((nq - 1,)), sem((nq - 1,)),
            sem((ng - 1,)), sem((ng - 1,)), sem((ng - 1,)), sem((ng - 1,)),
            sem((nq - 1,)), sem((nq - 1,)), sem(()), sem(()),
        ],
        compiler_params=pltpu.CompilerParams(
            collective_id=0, has_side_effects=True, vmem_limit_bytes=40 * 1024 * 1024
        ),
    )(col_index, live_counts, basis.reshape(n_rows, BS, width), stiffness, mass)
    return (stiff.reshape(n_rows * BS, width), massb.reshape(n_rows * BS, width), kgram, mgram)


def solution(mesh):
    in_specs = (
        P(("loop", "grp"), None),
        P(("loop", "grp"), None, None),
        P(("loop", "grp"), None, None),
        P(("loop", "grp"), None),
        P(("loop", "grp")),
    )
    out_specs = (P(("loop", "grp"), None), P(("loop", "grp"), None), P(), P())
    return jax.shard_map(
        on_device, mesh=mesh, in_specs=in_specs, out_specs=out_specs, check_vma=False
    )
```

```python
import functools

import jax
import jax.numpy as jnp
from jax import lax
from jax.experimental import pallas as pl
from jax.experimental.pallas import tpu as pltpu
from jax.sharding import PartitionSpec as P

BS = 64
NB = 16
LOCAL = 6
LANES = 128
GROUPS = 4
HALVES = 2
CHUNKS = 2
MESH = pl.DeviceIdType.MESH
BF16 = jnp.bfloat16
F32 = jnp.float32

SIB, AHEAD, FWD, BEHIND = range(4)


def fused_kernel(
    nl, ng, split, factor,
    col, live, basis, k_hbm, m_hbm,
    sbk, sbm, kgram, mgram,
    k_raw, m_raw, k_scr, m_scr, lhs, own, panels0, panels1, basis_t, acc, tmp, stiff, massb,
    part, land_c, half, land_q, red, land_g, res,
    own_sem, k_sem, m_sem, out_sem, s_sib, r_sib, s_ahead, r_ahead, s_behind, r_behind, s_fwd, r_fwd,
    s_a1, r_a1, s_a2, r_a2, s_b, r_b, s_c, r_c, s_d1, r_d1, s_d2, r_d2,
):
    me_l, me_g = lax.axis_index("loop"), lax.axis_index("grp")
    nq = nl // 2
    me_q, me_c = me_l // 2, lax.rem(me_l, 2)
    n_rows = k_raw.shape[0]
    panels = (panels0, panels1)
    per = n_rows // GROUPS
    chunk = n_rows // CHUNKS
    sibling = (2 * me_q + 1 - me_c, me_g)
    whole = split == 1

    def chip(d):
        return (2 * lax.rem(me_q + d, nq) + me_c, me_g)

    def grp(d):
        return (me_l, lax.rem(me_g + d, ng))

    def send(src, dst, s, r, dev):
        return pltpu.make_async_remote_copy(
            src_ref=src, dst_ref=dst, send_sem=s, recv_sem=r, device_id=dev, device_id_type=MESH)

    def lanes(w):
        return pl.ds(w * LANES, LANES)

    own_loads = [
        pltpu.make_async_copy(basis.at[:, :, lanes(w)], own.at[w, pl.ds(0, n_rows)], own_sem.at[w])
        for w in range(HALVES)
    ]
    for c in own_loads:
        c.start()
    barrier = pltpu.get_barrier_semaphore()
    pl.semaphore_signal(barrier, inc=1, device_id=sibling, device_id_type=MESH)
    for d in range(1, nq):
        pl.semaphore_signal(barrier, inc=1, device_id=chip(d), device_id_type=MESH)
    for d in range(1, ng):
        pl.semaphore_signal(barrier, inc=1, device_id=grp(d), device_id_type=MESH)
    loads = []
    for t in range(GROUPS):
        span = pl.ds(t * per, per)
        pair = (
            pltpu.make_async_copy(k_hbm.at[span], k_raw.at[span], k_sem.at[t]),
            pltpu.make_async_copy(m_hbm.at[span], m_raw.at[span], m_sem.at[t]),
        )
        for c in pair:
            c.start()
        loads.append(pair)
    zero = jnp.zeros((BS, LANES), BF16)
    for w in range(HALVES):
        own[w, n_rows] = zero
        for s in range(panels[w].shape[0]):
            panels[w][s, n_rows] = zero
    for c in own_loads:
        c.wait()
    pl.semaphore_wait(barrier, 1 + (nq - 1) + (ng - 1))

    two_ways = nq > 2
    far = AHEAD if not two_ways else jnp.where(me_c == 0, AHEAD, BEHIND)
    arrive, forward, sib = [], [], []
    for w in range(HALVES):
        for t in range(CHUNKS):
            span = pl.ds(t * chunk, chunk)
            src = own.at[w, span]
            pair = [send(src, panels[w].at[AHEAD, span], s_ahead.at[w, t], r_ahead.at[w, t], chip(nq - 1))]
            if two_ways:
                pair.append(send(src, panels[w].at[BEHIND, span], s_behind.at[w, t], r_behind.at[w, t], chip(1)))
            for c in pair:
                c.start()
            arrive.append(pair)
            forward.append(
                send(panels[w].at[far, span], panels[w].at[FWD, span], s_fwd.at[w, t], r_fwd.at[w, t], sibling))
        sib.append(
            send(own.at[w, pl.ds(0, n_rows)], panels[w].at[SIB, pl.ds(0, n_rows)], s_sib.at[w], r_sib.at[w], sibling))
        sib[w].start()

    def pass_on(i):
        for c in arrive[i]:
            c.wait_recv()
        forward[i].start()

    low = lax.broadcasted_iota(jnp.int32, (BS // 2, LANES), 1) < BS

    def relayout(raw, scr, r, base):
        for p in range(BS // 2):
            scr[p * NB : (p + 1) * NB, :] = raw[r, :, p * LANES : (p + 1) * LANES].astype(F32)
        for j in range(NB // 2):
            even = scr[pl.ds(2 * j, BS // 2, stride=NB), :]
            odd = scr[pl.ds(2 * j + 1, BS // 2, stride=NB), :]
            first = jnp.where(low, even, pltpu.roll(odd, BS, 1))
            second = jnp.where(low, pltpu.roll(even, BS, 1), odd)
            at = slice(j * LANES, (j + 1) * LANES)
            lhs[r, base : base + BS // 2, at] = first.astype(BF16)
            lhs[r, base + BS // 2 : base + BS, at] = second.astype(BF16)

    for t in range(GROUPS):
        for c in loads[t]:
            c.wait()

        def rows(r, carry):
            relayout(k_raw, k_scr, r, 0)
            relayout(m_raw, m_scr, r, BS)
            return carry

        lax.fori_loop(t * per, (t + 1) * per, rows, 0)
        if t % 2 == 1 and t // 2 < CHUNKS:
            pass_on(t // 2)

    def block(r, s):
        return jnp.where(s < live[r], col[r, s], n_rows)

    def local_rows(r, carry):
        for w in range(HALVES):
            rhs = jnp.concatenate([own[w, block(r, s)] for s in range(LOCAL)], 0)
            acc[w, r] = jnp.dot(lhs[r, :, : LOCAL * BS], rhs, preferred_element_type=F32)
        return carry

    lax.fori_loop(0, n_rows, local_rows, 0)
    for w in range(HALVES):
        basis_t[w * LANES : (w + 1) * LANES, :] = own[w, :n_rows].reshape(n_rows * BS, LANES).T

    plus = jnp.where(me_c == 0, SIB, FWD)
    minus = jnp.where(me_c == 0, FWD, SIB)
    back = BEHIND if two_ways else AHEAD
    owners = [plus] * 3 + [minus] * 3 + [AHEAD] * 2 + [back] * 2
    step = part.shape[4]
    pieces = 2 * HALVES * LANES // step // 2
    outs = []

    def products(w):
        sib[w].wait()
        for t in range(CHUNKS):
            for c in arrive[w * CHUNKS + t]:
                c.wait_send()
            forward[w * CHUNKS + t].wait()

        def remote_rows(r, carry):
            rhs = jnp.concatenate([panels[w][o, block(r, LOCAL + s)] for s, o in enumerate(owners)], 0)
            out = acc[w, r] + jnp.dot(lhs[r, :, LOCAL * BS :], rhs, preferred_element_type=F32)
            h = BS // 2
            for m, dst in enumerate((stiff, massb)):
                tmp[m, pl.ds(0, h, stride=2), :] = out[m * BS : m * BS + h]
                tmp[m, pl.ds(1, h, stride=2), :] = out[m * BS + h : (m + 1) * BS]
                dst[w, r] = tmp[m].astype(BF16)
            return carry

        lax.fori_loop(0, n_rows, remote_rows, 0)
        for m, (src, dst) in enumerate(((stiff, sbk), (massb, sbm))):
            gram = jnp.dot(basis_t[...], src[w].reshape(n_rows * BS, LANES), preferred_element_type=F32)
            for i in range(pieces):
                n = m * pieces + i
                part[w, n // (2 * split), n // split % 2, n % split] = gram[i * step : (i + 1) * step]

    def store(w):
        for m, (src, dst) in enumerate(((stiff, sbk), (massb, sbm))):
            c = pltpu.make_async_copy(src.at[w], dst.at[:, :, lanes(w)], out_sem.at[w, m])
            c.start()
            outs.append(c)

    def stages(w):
        def to_sibling():
            return [send(part.at[w, :, 1 - me_c], land_c.at[w], s_a1.at[w], r_a1.at[w], sibling)]

        def to_chips():
            half[w] = part[w, :, me_c] + land_c[w]
            return [
                send(half.at[w, lax.rem(me_q + d, nq)], land_q.at[w, d - 1], s_a2.at[w, d - 1], r_a2.at[w, d - 1], chip(d))
                for d in range(1, nq)
            ]

        def to_group():
            total = half[w, me_q]
            for d in range(1, nq):
                total = total + land_q[w, d - 1]
            red[w] = total
            return [
                send(
                    red.at[w, 0] if whole else red.at[w, lax.rem(me_g + d, ng)],
                    land_g.at[w, d - 1], s_b.at[w, d - 1], r_b.at[w, d - 1], grp(d))
                for d in range(1, ng)
            ]

        def from_group():
            if whole:
                land_g[w, ng - 1] = red[w, 0]
                mine = land_g[w, lax.rem(me_g + ng - 1, ng)]
                for g in range(1, ng):
                    mine = mine + land_g[w, lax.rem(me_g - g + 2 * ng - 1, ng)]
                res[w, me_q, me_c, 0] = mine * factor
                return []
            mine = red[w, me_g]
            for d in range(1, ng):
                mine = mine + land_g[w, d - 1]
            res[w, me_q, me_c, me_g] = mine * factor
            piece = res.at[w, me_q, me_c, me_g]
            return [send(piece, piece, s_c.at[w, d - 1], r_c.at[w, d - 1], grp(d)) for d in range(1, ng)]

        def from_chips():
            piece = res.at[w, me_q, me_c]
            return [send(piece, piece, s_d1.at[w, d - 1], r_d1.at[w, d - 1], chip(d)) for d in range(1, nq)]

        def from_sibling():
            piece = res.at[w, :, me_c]
            return [send(piece, piece, s_d2.at[w], r_d2.at[w], sibling)]

        for stage in (to_sibling, to_chips, to_group, from_group, from_chips, from_sibling):
            copies = stage()
            for c in copies:
                c.start()
            yield
            for c in copies:
                c.wait()
        for m, dst in enumerate((kgram, mgram)):
            for i in range(pieces):
                n = m * pieces + i
                dst[i * step : (i + 1) * step, w * LANES : (w + 1) * LANES] = res[
                    w, n // (2 * split), n // split % 2, n % split]

    first, second = stages(0), stages(1)
    products(0)
    next(first)
    store(0)
    pass_on(CHUNKS)
    next(first)
    for t in range(1, CHUNKS):
        pass_on(CHUNKS + t)
    next(first)
    products(1)
    next(second)
    store(1)
    for _ in range(3):
        next(first)
        next(second)
    next(first, None)
    for _ in second:
        pass
    for c in outs:
        c.wait()


def copy_kernel(*refs):
    n = len(refs) // 2
    copies = [pltpu.make_async_copy(refs[i], refs[n + i], refs[-1].at[i]) for i in range(n)]
    for c in copies:
        c.start()
    for c in copies:
        c.wait()


def on_device(basis, stiffness, mass, col_index, live_counts):
    nl, ng = lax.axis_size("loop"), lax.axis_size("grp")
    nq = nl // 2
    n_rows = stiffness.shape[0]
    width = basis.shape[1]
    step = 2 * width // nl
    split = ng if step % (8 * ng) == 0 else 1
    step = step // split
    factor = 1.0 / (basis.shape[0] * nl * ng) ** 0.5
    vmem, smem, hbm = (pl.BlockSpec(memory_space=s) for s in (pltpu.VMEM, pltpu.SMEM, pltpu.HBM))
    sem = pltpu.SemaphoreType.DMA
    sb = jax.ShapeDtypeStruct((n_rows, BS, width), BF16)
    gram = jax.ShapeDtypeStruct((width, width), F32)
    panel = pltpu.VMEM((4 if nq > 2 else 3, n_rows + 1, BS, LANES), BF16)

    def f32(*shape):
        return pltpu.VMEM(shape, F32)

    def sems(n, *shape):
        return [sem(shape)] * n

    outs = pl.pallas_call(
        functools.partial(fused_kernel, nl, ng, split, factor),
        out_shape=(sb, sb, gram, gram),
        in_specs=[smem, smem, hbm, hbm, hbm],
        out_specs=(hbm, hbm, vmem, vmem),
        scratch_shapes=[
            pltpu.VMEM(stiffness.shape, BF16),
            pltpu.VMEM(mass.shape, BF16),
            f32(NB * BS // 2, LANES),
            f32(NB * BS // 2, LANES),
            pltpu.VMEM((n_rows, 2 * BS, NB * BS), BF16),
            pltpu.VMEM((HALVES, n_rows + 1, BS, LANES), BF16),
            panel,
            panel,
            pltpu.VMEM((width, n_rows * BS), BF16),
            f32(HALVES, n_rows, 2 * BS, LANES),
            f32(2, BS, LANES),
            pltpu.VMEM((HALVES, n_rows, BS, LANES), BF16),
            pltpu.VMEM((HALVES, n_rows, BS, LANES), BF16),
            f32(HALVES, nq, 2, split, step, LANES),
            f32(HALVES, nq, split, step, LANES),
            f32(HALVES, nq, split, step, LANES),
            f32(HALVES, nq - 1, split, step, LANES),
            f32(HALVES, split, step, LANES),
            f32(HALVES, ng, step, LANES),
            f32(HALVES, nq, 2, split, step, LANES),
            *sems(1, HALVES), *sems(2, GROUPS), *sems(1, HALVES, 2), *sems(2, HALVES), *sems(6, HALVES, CHUNKS),
            *sems(2, HALVES), *sems(2, HALVES, nq - 1), *sems(4, HALVES, ng - 1),
            *sems(2, HALVES, nq - 1), *sems(2, HALVES),
        ],
        compiler_params=pltpu.CompilerParams(
            collective_id=0, has_side_effects=True, vmem_limit_bytes=60 * 1024 * 1024
        ),
    )(col_index, live_counts, basis.reshape(n_rows, BS, width), stiffness, mass)
    stiff, massb, kgram, mgram = pl.pallas_call(
        copy_kernel,
        out_shape=(sb, sb, gram, gram),
        in_specs=[hbm] * 4,
        out_specs=(hbm,) * 4,
        scratch_shapes=[sem((4,))],
    )(*outs)
    return (stiff.reshape(n_rows * BS, width), massb.reshape(n_rows * BS, width), kgram, mgram)


def solution(mesh):
    in_specs = (
        P(("loop", "grp"), None),
        P(("loop", "grp"), None, None),
        P(("loop", "grp"), None, None),
        P(("loop", "grp"), None),
        P(("loop", "grp")),
    )
    out_specs = (P(("loop", "grp"), None), P(("loop", "grp"), None), P(), P())
    return jax.shard_map(
        on_device, mesh=mesh, in_specs=in_specs, out_specs=out_specs, check_vma=False
    )
```

```python
import functools

import jax
import jax.numpy as jnp
from jax import lax
from jax.experimental import pallas as pl
from jax.experimental.pallas import tpu as pltpu
from jax.sharding import PartitionSpec as P

BS = 64
NB = 16
LOCAL = 6
LANES = 128
GROUPS = 4
MESH = pl.DeviceIdType.MESH
BF16 = jnp.bfloat16
F32 = jnp.float32

SIB, AHEAD, FWD, BEHIND = range(4)


def fused_kernel(
    nl, ng, split, factor,
    col, live, basis, k_hbm, m_hbm,
    sbk, sbm, kgram, mgram,
    k_raw, m_raw, k_scr, m_scr, lhs, own, panels, basis_t, acc, tmp,
    part, land_c, half, land_q, red, land_g, res,
    own_sem, k_sem, m_sem, s_sib, r_sib, s_ahead, r_ahead, s_behind, r_behind, s_fwd, r_fwd,
    s_a1, r_a1, s_a2, r_a2, s_b, r_b, s_c, r_c, s_d1, r_d1, s_d2, r_d2,
):
    me_l, me_g = lax.axis_index("loop"), lax.axis_index("grp")
    nq = nl // 2
    me_q, me_c = me_l // 2, lax.rem(me_l, 2)
    n_rows = k_raw.shape[0]
    width = basis.shape[2]
    per = n_rows // GROUPS
    sibling = (2 * me_q + 1 - me_c, me_g)

    def chip(d):
        return (2 * lax.rem(me_q + d, nq) + me_c, me_g)

    def grp(d):
        return (me_l, lax.rem(me_g + d, ng))

    def send(src, dst, s, r, dev):
        return pltpu.make_async_remote_copy(
            src_ref=src, dst_ref=dst, send_sem=s, recv_sem=r, device_id=dev, device_id_type=MESH)

    own_load = pltpu.make_async_copy(basis, own.at[pl.ds(0, n_rows)], own_sem)
    own_load.start()
    loads = []
    for t in range(GROUPS):
        span = pl.ds(t * per, per)
        pair = (
            pltpu.make_async_copy(k_hbm.at[span], k_raw.at[span], k_sem.at[t]),
            pltpu.make_async_copy(m_hbm.at[span], m_raw.at[span], m_sem.at[t]),
        )
        for c in pair:
            c.start()
        loads.append(pair)

    barrier = pltpu.get_barrier_semaphore()
    pl.semaphore_signal(barrier, inc=1, device_id=sibling, device_id_type=MESH)
    for d in range(1, nq):
        pl.semaphore_signal(barrier, inc=1, device_id=chip(d), device_id_type=MESH)
    for d in range(1, ng):
        pl.semaphore_signal(barrier, inc=1, device_id=grp(d), device_id_type=MESH)
    pl.semaphore_wait(barrier, 1 + (nq - 1) + (ng - 1))

    two_ways = nq > 2
    ahead, behind, forward = [], [], []
    far = AHEAD if not two_ways else jnp.where(me_c == 0, AHEAD, BEHIND)
    for t in range(GROUPS):
        span = pl.ds(t * per, per)
        c = send(basis.at[span], panels.at[AHEAD, span], s_ahead.at[t], r_ahead.at[t], chip(nq - 1))
        c.start()
        ahead.append(c)
        if two_ways:
            c = send(basis.at[span], panels.at[BEHIND, span], s_behind.at[t], r_behind.at[t], chip(1))
            c.start()
            behind.append(c)
        forward.append(send(panels.at[far, span], panels.at[FWD, span], s_fwd.at[t], r_fwd.at[t], sibling))
    sib = send(basis, panels.at[SIB, pl.ds(0, n_rows)], s_sib, r_sib, sibling)
    sib.start()

    own[n_rows] = jnp.zeros((BS, width), BF16)
    for s in range(panels.shape[0]):
        panels[s, n_rows] = jnp.zeros((BS, width), BF16)

    low = lax.broadcasted_iota(jnp.int32, (BS // 2, LANES), 1) < BS

    def relayout(raw, scr, r, base):
        for p in range(BS // 2):
            scr[p * NB : (p + 1) * NB, :] = raw[r, :, p * LANES : (p + 1) * LANES].astype(F32)
        for j in range(NB // 2):
            even = scr[pl.ds(2 * j, BS // 2, stride=NB), :]
            odd = scr[pl.ds(2 * j + 1, BS // 2, stride=NB), :]
            first = jnp.where(low, even, pltpu.roll(odd, BS, 1))
            second = jnp.where(low, pltpu.roll(even, BS, 1), odd)
            lanes = slice(j * LANES, (j + 1) * LANES)
            lhs[r, base : base + BS // 2, lanes] = first.astype(BF16)
            lhs[r, base + BS // 2 : base + BS, lanes] = second.astype(BF16)

    for t in range(GROUPS):
        for c in loads[t]:
            c.wait()

        def rows(r, carry):
            relayout(k_raw, k_scr, r, 0)
            relayout(m_raw, m_scr, r, BS)
            return carry

        lax.fori_loop(t * per, (t + 1) * per, rows, 0)
        ahead[t].wait_recv()
        if two_ways:
            behind[t].wait_recv()
        forward[t].start()

    def block(r, s):
        return jnp.where(s < live[r], col[r, s], n_rows)

    own_load.wait()

    def local_rows(r, carry):
        rhs = jnp.concatenate([own[block(r, s)] for s in range(LOCAL)], 0)
        acc[r] = jnp.dot(lhs[r, :, : LOCAL * BS], rhs, preferred_element_type=F32)
        return carry

    lax.fori_loop(0, n_rows, local_rows, 0)
    basis_t[...] = own[:n_rows].reshape(n_rows * BS, width).T

    sib.wait()
    for t in range(GROUPS):
        ahead[t].wait_send()
        if two_ways:
            behind[t].wait_send()
        forward[t].wait()

    plus = jnp.where(me_c == 0, SIB, FWD)
    minus = jnp.where(me_c == 0, FWD, SIB)
    back = BEHIND if two_ways else AHEAD
    owners = [plus] * 3 + [minus] * 3 + [AHEAD] * 2 + [back] * 2

    def remote_rows(r, carry):
        rhs = jnp.concatenate([panels[o, block(r, LOCAL + s)] for s, o in enumerate(owners)], 0)
        out = acc[r] + jnp.dot(lhs[r, :, LOCAL * BS :], rhs, preferred_element_type=F32)
        h = BS // 2
        for m, dst in enumerate((sbk, sbm)):
            for w in range(width // LANES):
                i = m * (width // LANES) + w
                lanes = slice(w * LANES, (w + 1) * LANES)
                tmp[i, pl.ds(0, h, stride=2), :] = out[m * BS : m * BS + h, lanes]
                tmp[i, pl.ds(1, h, stride=2), :] = out[m * BS + h : (m + 1) * BS, lanes]
                dst[r, :, lanes] = tmp[i].astype(BF16)
        return carry

    lax.fori_loop(0, n_rows, remote_rows, 0)

    step = part.shape[3]
    pieces = width // step
    for m, src in enumerate((sbk, sbm)):
        gram = jnp.dot(basis_t[...], src[...].reshape(n_rows * BS, width), preferred_element_type=F32)
        for i in range(pieces):
            n = m * pieces + i
            part[n // (2 * split), n // split % 2, n % split] = gram[i * step : (i + 1) * step]

    c = send(part.at[:, 1 - me_c], land_c, s_a1, r_a1, sibling)
    c.start()
    c.wait()
    half[...] = part[:, me_c] + land_c[...]
    whole = split == 1
    chips = [
        [
            send(
                half.at[lax.rem(me_q + d, nq), g], land_q.at[d - 1, g], s_a2.at[d - 1, i], r_a2.at[d - 1, i], chip(d))
            for d in range(1, nq)
        ]
        for i in range(split)
        for g in [lax.rem(me_g + 1 + i, split)]
    ]
    for pair in chips:
        for c in pair:
            c.start()
    copies = []
    for i in range(split):
        g = lax.rem(me_g + 1 + i, split)
        total = half[me_q, g]
        for d in range(1, nq):
            chips[i][d - 1].wait_recv()
            total = total + land_q[d - 1, g]
        red[g] = total
        if not whole and i < ng - 1:
            copies.append(send(red.at[g], land_g.at[i], s_b.at[i], r_b.at[i], grp(i + 1)))
            copies[-1].start()
    if whole:
        copies = [send(red.at[0], land_g.at[d - 1], s_b.at[d - 1], r_b.at[d - 1], grp(d)) for d in range(1, ng)]
        for c in copies:
            c.start()
    for pair in chips:
        for c in pair:
            c.wait_send()
    for c in copies:
        c.wait()
    if whole:
        land_g[ng - 1] = red[0]
        mine = land_g[lax.rem(me_g + ng - 1, ng)]
        for g in range(1, ng):
            mine = mine + land_g[lax.rem(me_g - g + 2 * ng - 1, ng)]
        res[me_q, me_c, 0] = mine * factor
    else:
        mine = red[me_g]
        for d in range(1, ng):
            mine = mine + land_g[d - 1]
        res[me_q, me_c, me_g] = mine * factor
        piece = res.at[me_q, me_c, me_g]
        gather = [send(piece, piece, s_c.at[d - 1], r_c.at[d - 1], grp(d)) for d in range(1, ng)]
        for c in gather:
            c.start()
    copies = []
    for i in range(split):
        if i > 0:
            gather[i - 1].wait_recv()
        piece = res.at[me_q, me_c, lax.rem(me_g + split - i, split)]
        for d in range(1, nq):
            copies.append(send(piece, piece, s_d1.at[d - 1, i], r_d1.at[d - 1, i], chip(d)))
            copies[-1].start()
    if not whole:
        for c in gather:
            c.wait_send()
    for c in copies:
        c.wait()
    piece = res.at[:, me_c]
    c = send(piece, piece, s_d2, r_d2, sibling)
    c.start()
    c.wait()
    for m, dst in enumerate((kgram, mgram)):
        for i in range(pieces):
            n = m * pieces + i
            dst[i * step : (i + 1) * step, :] = res[n // (2 * split), n // split % 2, n % split]


def copy_kernel(*refs):
    n = len(refs) // 2
    copies = [pltpu.make_async_copy(refs[i], refs[n + i], refs[-1].at[i]) for i in range(n)]
    for c in copies:
        c.start()
    for c in copies:
        c.wait()


def on_device(basis, stiffness, mass, col_index, live_counts):
    nl, ng = lax.axis_size("loop"), lax.axis_size("grp")
    nq = nl // 2
    n_rows = stiffness.shape[0]
    width = basis.shape[1]
    step = 2 * width // nl
    split = ng if step % (8 * ng) == 0 else 1
    step = step // split
    factor = 1.0 / (basis.shape[0] * nl * ng) ** 0.5
    vmem, smem, hbm = (pl.BlockSpec(memory_space=s) for s in (pltpu.VMEM, pltpu.SMEM, pltpu.HBM))
    sem = pltpu.SemaphoreType.DMA
    sb = jax.ShapeDtypeStruct((n_rows, BS, width), BF16)
    gram = jax.ShapeDtypeStruct((width, width), F32)
    outs = pl.pallas_call(
        functools.partial(fused_kernel, nl, ng, split, factor),
        out_shape=(sb, sb, gram, gram),
        in_specs=[smem, smem, hbm, hbm, hbm],
        out_specs=(vmem,) * 4,
        scratch_shapes=[
            pltpu.VMEM(stiffness.shape, BF16),
            pltpu.VMEM(mass.shape, BF16),
            pltpu.VMEM((NB * BS // 2, LANES), F32),
            pltpu.VMEM((NB * BS // 2, LANES), F32),
            pltpu.VMEM((n_rows, 2 * BS, NB * BS), BF16),
            pltpu.VMEM((n_rows + 1, BS, width), BF16),
            pltpu.VMEM((4 if nq > 2 else 3, n_rows + 1, BS, width), BF16),
            pltpu.VMEM((width, n_rows * BS), BF16),
            pltpu.VMEM((n_rows, 2 * BS, width), F32),
            pltpu.VMEM((2 * width // LANES, BS, LANES), F32),
            pltpu.VMEM((nq, 2, split, step, width), F32),
            pltpu.VMEM((nq, split, step, width), F32),
            pltpu.VMEM((nq, split, step, width), F32),
            pltpu.VMEM((nq - 1, split, step, width), F32),
            pltpu.VMEM((split, step, width), F32),
            pltpu.VMEM((ng, step, width), F32),
            pltpu.VMEM((nq, 2, split, step, width), F32),
            sem(()), sem((GROUPS,)), sem((GROUPS,)), sem(()), sem(()),
            sem((GROUPS,)), sem((GROUPS,)), sem((GROUPS,)), sem((GROUPS,)), sem((GROUPS,)), sem((GROUPS,)),
            sem(()), sem(()), sem((nq - 1, split)), sem((nq - 1, split)),
            sem((ng - 1,)), sem((ng - 1,)), sem((ng - 1,)), sem((ng - 1,)),
            sem((nq - 1, split)), sem((nq - 1, split)), sem(()), sem(()),
        ],
        compiler_params=pltpu.CompilerParams(
            collective_id=0, has_side_effects=True, vmem_limit_bytes=60 * 1024 * 1024
        ),
    )(col_index, live_counts, basis.reshape(n_rows, BS, width), stiffness, mass)
    stiff, massb, kgram, mgram = pl.pallas_call(
        copy_kernel,
        out_shape=(sb, sb, gram, gram),
        in_specs=[vmem] * 4,
        out_specs=(hbm,) * 4,
        scratch_shapes=[sem((4,))],
    )(*outs)
    return (stiff.reshape(n_rows * BS, width), massb.reshape(n_rows * BS, width), kgram, mgram)


def solution(mesh):
    in_specs = (
        P(("loop", "grp"), None),
        P(("loop", "grp"), None, None),
        P(("loop", "grp"), None, None),
        P(("loop", "grp"), None),
        P(("loop", "grp")),
    )
    out_specs = (P(("loop", "grp"), None), P(("loop", "grp"), None), P(), P())
    return jax.shard_map(
        on_device, mesh=mesh, in_specs=in_specs, out_specs=out_specs, check_vma=False
    )
```

```python
import functools

import jax
import jax.numpy as jnp
from jax import lax
from jax.experimental import pallas as pl
from jax.experimental.pallas import tpu as pltpu
from jax.sharding import PartitionSpec as P

BS = 64
NB = 16
LOCAL = 6
LANES = 128
GROUPS = 4
MESH = pl.DeviceIdType.MESH
BF16 = jnp.bfloat16
F32 = jnp.float32

SIB, AHEAD, FWD, BEHIND = range(4)


def fused_kernel(
    nl, ng, split, factor,
    col, live, basis, k_hbm, m_hbm,
    sbk, sbm, kgram, mgram,
    k_raw, m_raw, k_scr, m_scr, lhs, own, panels, basis_t, acc, tmp,
    part, land_c, half, land_q, red, land_g, res,
    own_sem, k_sem, m_sem, s_sib, r_sib, s_ahead, r_ahead, s_behind, r_behind, s_fwd, r_fwd,
    s_a1, r_a1, s_a2, r_a2, s_b, r_b, s_c, r_c, s_d1, r_d1, s_d2, r_d2,
):
    me_l, me_g = lax.axis_index("loop"), lax.axis_index("grp")
    nq = nl // 2
    me_q, me_c = me_l // 2, lax.rem(me_l, 2)
    n_rows = k_raw.shape[0]
    width = basis.shape[2]
    per = n_rows // GROUPS
    sibling = (2 * me_q + 1 - me_c, me_g)

    def chip(d):
        return (2 * lax.rem(me_q + d, nq) + me_c, me_g)

    def grp(d):
        return (me_l, lax.rem(me_g + d, ng))

    def send(src, dst, s, r, dev):
        return pltpu.make_async_remote_copy(
            src_ref=src, dst_ref=dst, send_sem=s, recv_sem=r, device_id=dev, device_id_type=MESH)

    own_load = pltpu.make_async_copy(basis, own.at[pl.ds(0, n_rows)], own_sem)
    own_load.start()
    loads = []
    for t in range(GROUPS):
        span = pl.ds(t * per, per)
        pair = (
            pltpu.make_async_copy(k_hbm.at[span], k_raw.at[span], k_sem.at[t]),
            pltpu.make_async_copy(m_hbm.at[span], m_raw.at[span], m_sem.at[t]),
        )
        for c in pair:
            c.start()
        loads.append(pair)

    barrier = pltpu.get_barrier_semaphore()
    pl.semaphore_signal(barrier, inc=1, device_id=sibling, device_id_type=MESH)
    for d in range(1, nq):
        pl.semaphore_signal(barrier, inc=1, device_id=chip(d), device_id_type=MESH)
    for d in range(1, ng):
        pl.semaphore_signal(barrier, inc=1, device_id=grp(d), device_id_type=MESH)
    pl.semaphore_wait(barrier, 1 + (nq - 1) + (ng - 1))

    two_ways = nq > 2
    ahead, behind, forward = [], [], []
    far = AHEAD if not two_ways else jnp.where(me_c == 0, AHEAD, BEHIND)
    for t in range(GROUPS):
        span = pl.ds(t * per, per)
        c = send(basis.at[span], panels.at[AHEAD, span], s_ahead.at[t], r_ahead.at[t], chip(nq - 1))
        c.start()
        ahead.append(c)
        if two_ways:
            c = send(basis.at[span], panels.at[BEHIND, span], s_behind.at[t], r_behind.at[t], chip(1))
            c.start()
            behind.append(c)
        forward.append(send(panels.at[far, span], panels.at[FWD, span], s_fwd.at[t], r_fwd.at[t], sibling))
    sib = send(basis, panels.at[SIB, pl.ds(0, n_rows)], s_sib, r_sib, sibling)
    sib.start()

    own[n_rows] = jnp.zeros((BS, width), BF16)
    for s in range(panels.shape[0]):
        panels[s, n_rows] = jnp.zeros((BS, width), BF16)

    low = lax.broadcasted_iota(jnp.int32, (BS // 2, LANES), 1) < BS

    def relayout(raw, scr, r, base):
        for p in range(BS // 2):
            scr[p * NB : (p + 1) * NB, :] = raw[r, :, p * LANES : (p + 1) * LANES].astype(F32)
        for j in range(NB // 2):
            even = scr[pl.ds(2 * j, BS // 2, stride=NB), :]
            odd = scr[pl.ds(2 * j + 1, BS // 2, stride=NB), :]
            first = jnp.where(low, even, pltpu.roll(odd, BS, 1))
            second = jnp.where(low, pltpu.roll(even, BS, 1), odd)
            lanes = slice(j * LANES, (j + 1) * LANES)
            lhs[r, base : base + BS // 2, lanes] = first.astype(BF16)
            lhs[r, base + BS // 2 : base + BS, lanes] = second.astype(BF16)

    for t in range(GROUPS):
        for c in loads[t]:
            c.wait()

        def rows(r, carry):
            relayout(k_raw, k_scr, r, 0)
            relayout(m_raw, m_scr, r, BS)
            return carry

        lax.fori_loop(t * per, (t + 1) * per, rows, 0)
        ahead[t].wait_recv()
        if two_ways:
            behind[t].wait_recv()
        forward[t].start()

    def block(r, s):
        return jnp.where(s < live[r], col[r, s], n_rows)

    own_load.wait()

    def local_rows(r, carry):
        rhs = jnp.concatenate([own[block(r, s)] for s in range(LOCAL)], 0)
        acc[r] = jnp.dot(lhs[r, :, : LOCAL * BS], rhs, preferred_element_type=F32)
        return carry

    lax.fori_loop(0, n_rows, local_rows, 0)
    basis_t[...] = own[:n_rows].reshape(n_rows * BS, width).T

    sib.wait()
    for t in range(GROUPS):
        ahead[t].wait_send()
        if two_ways:
            behind[t].wait_send()
        forward[t].wait()

    plus = jnp.where(me_c == 0, SIB, FWD)
    minus = jnp.where(me_c == 0, FWD, SIB)
    back = BEHIND if two_ways else AHEAD
    owners = [plus] * 3 + [minus] * 3 + [AHEAD] * 2 + [back] * 2

    def remote_rows(r, carry):
        rhs = jnp.concatenate([panels[o, block(r, LOCAL + s)] for s, o in enumerate(owners)], 0)
        out = acc[r] + jnp.dot(lhs[r, :, LOCAL * BS :], rhs, preferred_element_type=F32)
        h = BS // 2
        for m, dst in enumerate((sbk, sbm)):
            for w in range(width // LANES):
                i = m * (width // LANES) + w
                lanes = slice(w * LANES, (w + 1) * LANES)
                tmp[i, pl.ds(0, h, stride=2), :] = out[m * BS : m * BS + h, lanes]
                tmp[i, pl.ds(1, h, stride=2), :] = out[m * BS + h : (m + 1) * BS, lanes]
                dst[r, :, lanes] = tmp[i].astype(BF16)
        return carry

    lax.fori_loop(0, n_rows, remote_rows, 0)

    step = part.shape[3]
    pieces = width // step
    for m, src in enumerate((sbk, sbm)):
        gram = jnp.dot(basis_t[...], src[...].reshape(n_rows * BS, width), preferred_element_type=F32)
        for i in range(pieces):
            n = m * pieces + i
            part[n // (2 * split), n // split % 2, n % split] = gram[i * step : (i + 1) * step]

    c = send(part.at[:, 1 - me_c], land_c, s_a1, r_a1, sibling)
    c.start()
    c.wait()
    half[...] = part[:, me_c] + land_c[...]
    whole = split == 1
    chips = [
        [
            send(
                half.at[lax.rem(me_q + d, nq), g], land_q.at[d - 1, g], s_a2.at[d - 1, i], r_a2.at[d - 1, i], chip(d))
            for d in range(1, nq)
        ]
        for i in range(split)
        for g in [lax.rem(me_g + 1 + i, split)]
    ]
    for pair in chips:
        for c in pair:
            c.start()
    copies = []
    for i in range(split):
        g = lax.rem(me_g + 1 + i, split)
        total = half[me_q, g]
        for d in range(1, nq):
            chips[i][d - 1].wait_recv()
            total = total + land_q[d - 1, g]
        red[g] = total
        if not whole and i < ng - 1:
            copies.append(send(red.at[g], land_g.at[i], s_b.at[i], r_b.at[i], grp(i + 1)))
            copies[-1].start()
    if whole:
        copies = [send(red.at[0], land_g.at[d - 1], s_b.at[d - 1], r_b.at[d - 1], grp(d)) for d in range(1, ng)]
        for c in copies:
            c.start()
    for pair in chips:
        for c in pair:
            c.wait_send()
    for c in copies:
        c.wait()
    if whole:
        land_g[ng - 1] = red[0]
        mine = land_g[lax.rem(me_g + ng - 1, ng)]
        for g in range(1, ng):
            mine = mine + land_g[lax.rem(me_g - g + 2 * ng - 1, ng)]
        res[me_q, me_c, 0] = (mine * factor).astype(BF16)
    else:
        mine = red[me_g]
        for d in range(1, ng):
            mine = mine + land_g[d - 1]
        res[me_q, me_c, me_g] = (mine * factor).astype(BF16)
        piece = res.at[me_q, me_c, me_g]
        gather = [send(piece, piece, s_c.at[d - 1], r_c.at[d - 1], grp(d)) for d in range(1, ng)]
        for c in gather:
            c.start()
    copies = []
    for i in range(split):
        if i > 0:
            gather[i - 1].wait_recv()
        piece = res.at[me_q, me_c, lax.rem(me_g + split - i, split)]
        for d in range(1, nq):
            copies.append(send(piece, piece, s_d1.at[d - 1, i], r_d1.at[d - 1, i], chip(d)))
            copies[-1].start()
    if not whole:
        for c in gather:
            c.wait_send()
    for c in copies:
        c.wait()
    piece = res.at[:, me_c]
    c = send(piece, piece, s_d2, r_d2, sibling)
    c.start()
    c.wait()
    for m, dst in enumerate((kgram, mgram)):
        for i in range(pieces):
            n = m * pieces + i
            dst[i * step : (i + 1) * step, :] = res[n // (2 * split), n // split % 2, n % split].astype(F32)


def copy_kernel(*refs):
    n = len(refs) // 2
    copies = [pltpu.make_async_copy(refs[i], refs[n + i], refs[-1].at[i]) for i in range(n)]
    for c in copies:
        c.start()
    for c in copies:
        c.wait()


def on_device(basis, stiffness, mass, col_index, live_counts):
    nl, ng = lax.axis_size("loop"), lax.axis_size("grp")
    nq = nl // 2
    n_rows = stiffness.shape[0]
    width = basis.shape[1]
    step = 2 * width // nl
    split = ng if step % (8 * ng) == 0 else 1
    step = step // split
    factor = 1.0 / (basis.shape[0] * nl * ng) ** 0.5
    vmem, smem, hbm = (pl.BlockSpec(memory_space=s) for s in (pltpu.VMEM, pltpu.SMEM, pltpu.HBM))
    sem = pltpu.SemaphoreType.DMA
    sb = jax.ShapeDtypeStruct((n_rows, BS, width), BF16)
    gram = jax.ShapeDtypeStruct((width, width), F32)
    outs = pl.pallas_call(
        functools.partial(fused_kernel, nl, ng, split, factor),
        out_shape=(sb, sb, gram, gram),
        in_specs=[smem, smem, hbm, hbm, hbm],
        out_specs=(vmem,) * 4,
        scratch_shapes=[
            pltpu.VMEM(stiffness.shape, BF16),
            pltpu.VMEM(mass.shape, BF16),
            pltpu.VMEM((NB * BS // 2, LANES), F32),
            pltpu.VMEM((NB * BS // 2, LANES), F32),
            pltpu.VMEM((n_rows, 2 * BS, NB * BS), BF16),
            pltpu.VMEM((n_rows + 1, BS, width), BF16),
            pltpu.VMEM((4 if nq > 2 else 3, n_rows + 1, BS, width), BF16),
            pltpu.VMEM((width, n_rows * BS), BF16),
            pltpu.VMEM((n_rows, 2 * BS, width), F32),
            pltpu.VMEM((2 * width // LANES, BS, LANES), F32),
            pltpu.VMEM((nq, 2, split, step, width), F32),
            pltpu.VMEM((nq, split, step, width), F32),
            pltpu.VMEM((nq, split, step, width), F32),
            pltpu.VMEM((nq - 1, split, step, width), F32),
            pltpu.VMEM((split, step, width), F32),
            pltpu.VMEM((ng, step, width), F32),
            pltpu.VMEM((nq, 2, split, step, width), BF16),
            sem(()), sem((GROUPS,)), sem((GROUPS,)), sem(()), sem(()),
            sem((GROUPS,)), sem((GROUPS,)), sem((GROUPS,)), sem((GROUPS,)), sem((GROUPS,)), sem((GROUPS,)),
            sem(()), sem(()), sem((nq - 1, split)), sem((nq - 1, split)),
            sem((ng - 1,)), sem((ng - 1,)), sem((ng - 1,)), sem((ng - 1,)),
            sem((nq - 1, split)), sem((nq - 1, split)), sem(()), sem(()),
        ],
        compiler_params=pltpu.CompilerParams(
            collective_id=0, has_side_effects=True, vmem_limit_bytes=60 * 1024 * 1024
        ),
    )(col_index, live_counts, basis.reshape(n_rows, BS, width), stiffness, mass)
    stiff, massb, kgram, mgram = pl.pallas_call(
        copy_kernel,
        out_shape=(sb, sb, gram, gram),
        in_specs=[vmem] * 4,
        out_specs=(hbm,) * 4,
        scratch_shapes=[sem((4,))],
    )(*outs)
    return (stiff.reshape(n_rows * BS, width), massb.reshape(n_rows * BS, width), kgram, mgram)


def solution(mesh):
    in_specs = (
        P(("loop", "grp"), None),
        P(("loop", "grp"), None, None),
        P(("loop", "grp"), None, None),
        P(("loop", "grp"), None),
        P(("loop", "grp")),
    )
    out_specs = (P(("loop", "grp"), None), P(("loop", "grp"), None), P(), P())
    return jax.shard_map(
        on_device, mesh=mesh, in_specs=in_specs, out_specs=out_specs, check_vma=False
    )
```
